128 devices in a mesh: step: 8 (over y_lo, z), space: 16 (over x, y_hi, core).
Axes of the slice: x: 4, y: 4 (y_hi: 2, y_lo: 2; y = y_hi * 2 + y_lo), z: 4, core: 2. Of those that a mesh axis runs over, the one named last changes fastest.
Arguments:
- snapshots: float32 [8, 16, 256, 256], P('step', 'space'), may hold values from 0.25 to 2
- drift: bfloat16 [8, 3, 16, 256, 256], P('step', None, 'space'), may hold values from -3 to 3
- pair_table: int32 [16, 2], P('step'), may hold values from 0 to 7
- plan: int32 [16, 4], P('step'), may hold values from 0 to 7
Outputs:
- final_density: float32 [16, 16, 256, 256], P('step', 'space')
- adjoint_start: float32 [16, 16, 256, 256], P('step', 'space')
- drift_grad: float32 [8, 3, 16, 256, 256], P('step', None, 'space')
The draws below stay inside these ranges and needn't reach their ends.
All inputs are finite; a program needn't handle non-finite values.
Results may differ from the reference program's by a relative error of at most 0.0003.
Values may be sent and summed in bfloat16 or wider, within the bound.
No kernel may reach another device: no remote copies, remote signals or barrier semaphores. Data moves between devices by JAX's collectives and lax.ppermute only.
A program may use at most 64 MiB of HBM per device.

```python
import jax
import jax.numpy as jnp
from jax import lax

NX = 256
NY = 256
WIN = 4
NZ = 16
PAIRS = 16
STEPS = 8
SNAPS = 8


def touch_ends(entries, key, low, top_value):
    longest = entries.shape.index(max(entries.shape))
    spots = []
    for shift in (0, 1):
        where = [jax.random.randint(jax.random.fold_in(key, axis), (), 0, length) for axis, length in enumerate(entries.shape)]
        where[longest] = (where[longest] + shift) % entries.shape[longest]
        spots.append(tuple(where))
    return entries.at[spots[0]].set(low).at[spots[1]].set(top_value)


def steps_of(own_key, shape, shards, smallest, top_value):
    def one(dim, shards_of):
        draws = jax.random.uniform(jax.random.fold_in(jax.random.fold_in(own_key, 6), dim), (shards_of,), jnp.float32, smallest / len(shards), top_value / len(shards))
        return jnp.repeat(jnp.exp(draws), shape[dim] // shards_of).reshape((-1,) + (1,) * (len(shape) - dim - 1))

    factor_of = one(*shards[0])
    for cut in shards[1:]:
        factor_of = factor_of * one(*cut)
    return factor_of


def normal_values(rng, dims, spread, limit, pieces=(), held_as=jnp.bfloat16):
    drawn = spread * jax.random.normal(rng, dims, jnp.float32)
    if pieces:
        drawn = drawn * steps_of(rng, dims, pieces, -0.22, 0.18)
    return jnp.clip(drawn, -limit, limit).astype(held_as)


def setup_inputs(seed: int = 0) -> dict:
    streams_of = jax.random.split(jax.random.key(seed), 5)
    return {
        "snapshots": jnp.clip(0.25 + 1.75 * jax.random.uniform(streams_of[0], (SNAPS, NZ, NY, NX), jnp.float32) ** steps_of(streams_of[0], (SNAPS, NZ, NY, NX), ((0, 8), (1, 16)), -0.2, 0.2), 0.25, 2.0),
        "drift": normal_values(streams_of[1], (STEPS, 3, NZ, NY, NX), 0.5, 3.0, ((0, 8), (2, 16))),
        "pair_table": touch_ends(jax.random.randint(streams_of[2], (PAIRS, 2), 0, SNAPS), jax.random.fold_in(streams_of[2], 1), 0, SNAPS - 1).astype(jnp.int32),
        "plan": touch_ends(jax.random.randint(streams_of[3], (PAIRS, WIN), 0, STEPS), jax.random.fold_in(streams_of[3], 1), 0, STEPS - 1).astype(jnp.int32),
    }


time_step = 0.1
diffusion = 1.0


def pad_depth(field):
    return jnp.pad(field, ((1, 1), (0, 0), (0, 0)))


def diff_plane(field, axis):
    return (jnp.roll(field, -1, axis) - jnp.roll(field, 1, axis)) * 0.5


def diff_depth(padded):
    return (padded[2:] - padded[:-2]) * 0.5


def laplace(field, padded):
    total = padded[2:] + padded[:-2]
    total = total + jnp.roll(field, -1, 1) + jnp.roll(field, 1, 1)
    total = total + jnp.roll(field, -1, 2) + jnp.roll(field, 1, 2)
    return total - 6.0 * field


def forward_step(density, velocity):
    padded = pad_depth(density)
    flux_pad = pad_depth(velocity[2] * density)
    change = diffusion * laplace(density, padded) - diff_plane(velocity[0] * density, 2) - diff_plane(velocity[1] * density, 1) - diff_depth(flux_pad)
    return density + time_step * change


def adjoint_step(adjoint, velocity):
    padded = pad_depth(adjoint)
    slope_x = diff_plane(adjoint, 2)
    slope_y = diff_plane(adjoint, 1)
    slope_z = diff_depth(padded)
    change = diffusion * laplace(adjoint, padded) + velocity[0] * slope_x + velocity[1] * slope_y + velocity[2] * slope_z
    return adjoint + time_step * change, jnp.stack([slope_x, slope_y, slope_z])


def reference(snapshots, drift, pair_table, plan):
    def one_pair(totals, inputs):
        row_table, row_steps = inputs
        density = snapshots[row_table[0]]
        target = snapshots[row_table[1]]
        states = []
        for index in range(WIN):
            velocity = drift[row_steps[index]].astype(jnp.float32)
            states.append(density)
            density = forward_step(density, velocity)
        final = density
        adjoint = final - target
        for index in reversed(range(WIN)):
            velocity = drift[row_steps[index]].astype(jnp.float32)
            updated, slopes = adjoint_step(adjoint, velocity)
            term = time_step * states[index][None] * slopes
            totals = totals.at[row_steps[index]].add(term)
            adjoint = updated
        return totals, (final, adjoint)

    start = jnp.zeros((STEPS, 3, NZ, NY, NX), jnp.float32)
    totals, (finals, adjoints) = lax.scan(one_pair, start, (pair_table, plan))
    return finals, adjoints, totals
```

```python
import jax
import jax.numpy as jnp
from jax import lax
from jax.experimental import pallas as pl
from jax.experimental.pallas import tpu as pltpu
from jax.sharding import PartitionSpec as P

WIN = 4
NZ = 16
SIDE = 256
PAIRS = 16
STEPS = 8
OWN_Y = 32
OWN_X = 16
HALO = 2 * WIN
PITCH = OWN_X + 2 * HALO
GROUPS = (OWN_Y + 2 * HALO) // 4
OWN_LO = HALO // 4
OWN_HI = OWN_LO + OWN_Y // 4
IN_ROWS = 64
OUT_ROWS = 32
VREG = (8, 128)
TABLE_ROW = 60

time_step = 0.1
diffusion = 1.0
near = time_step * diffusion
keep = 1.0 - 6.0 * near
half = 0.5 * time_step


def lanes():
    return lax.broadcasted_iota(jnp.int32, VREG, 1)


def subs():
    return lax.broadcasted_iota(jnp.int32, VREG, 0)


def build_kernel(pairs_ref, plan_ref, snap_ref, drift_ref, out_ref, field_ref, wide_ref):
    for f in range(4):
        for h in range(2):
            cols = slice(128 * h, 128 * h + 128)
            plane = snap_ref[0, 0, :, cols] if f == 0 else drift_ref[0, f - 1, 0, :, cols].astype(jnp.float32)
            field_ref[f, h, 8:264, :] = plane
            field_ref[f, h, 0:8, :] = plane[248:256]
            field_ref[f, h, 264:288, :] = plane[0:24]
    lane = lax.broadcasted_iota(jnp.int32, (72, 128), 1)
    table = jnp.zeros(VREG, jnp.float32)
    for i in range(12):
        entry = pairs_ref[i // 2, i % 2] if i < 4 else plan_ref[(i - 4) // 4, (i - 4) % 4]
        table = jnp.where(lanes() == i, entry.astype(jnp.float32), table)
    upper = subs() < 4
    for bx in range(16):
        start = (OWN_X * bx - HALO) % SIDE
        side, offset = start // 128, start % 128
        for f in range(4):
            parts = []
            for j in range(4):
                shift = (PITCH * j - offset) % 128
                rows = pl.ds(j, 72, stride=4)
                part = pltpu.roll(field_ref[f, side, rows, :], shift, 1)
                if offset > 96:
                    other = pltpu.roll(field_ref[f, 1 - side, rows, :], shift, 1)
                    part = jnp.where(lane < PITCH * j + 128 - offset, part, other)
                parts.append(part)
            whole = jnp.where(
                lane < 64,
                jnp.where(lane < 32, parts[0], parts[1]),
                jnp.where(lane < 96, parts[2], parts[3]),
            )
            if f == 0:
                high = whole.astype(jnp.bfloat16).astype(jnp.float32)
                wide_ref[0] = high
                wide_ref[1] = whole - high
            else:
                wide_ref[f + 1] = whole
        for by in range(8):
            top = [wide_ref[f, 8 * by : 8 * by + 8, :] for f in range(5)]
            tail = [wide_ref[f, 8 * by + 8 : 8 * by + 16, :] for f in range(5)]
            ends = [
                jnp.where(upper, tail[0], pltpu.roll(tail[1], 4, 0)),
                jnp.where(upper, tail[2], pltpu.roll(tail[3], 4, 0)),
                jnp.where(upper, tail[4], table),
            ]
            out_ref[by * 16 + bx] = jnp.concatenate(top + ends, axis=0).astype(jnp.bfloat16)


def in_row(f, group):
    return 8 * f + group if group < 8 else 40 + 4 * f + group - 8


def window_kernel(in_ref, out_ref, rows_ref, snap_ref, drift_ref, rho_ref, lam_ref, grad_ref, table_ref):
    lane = lanes()
    sub = subs()
    zero = jnp.zeros(VREG, jnp.float32)
    first, last = sub == 0, sub == 7
    low, high = lane < 128 - PITCH, lane >= PITCH
    even = (lane % PITCH) < OWN_X

    def unpack(s, carry):
        for z in range(NZ):
            rows_ref[64 * z : 64 * z + 64, :] = in_ref[s * NZ + z].astype(jnp.float32)
        for zo in range(2):
            for g in range(GROUPS):
                parts = [rows_ref[pl.ds(512 * zo + in_row(f, g), 8, stride=64), :] for f in range(5)]
                snap_ref[s, zo * GROUPS + g] = parts[0] + parts[1]
                for c in range(3):
                    drift_ref[s, c, zo * GROUPS + g] = half * parts[2 + c]
        entries = jnp.where(sub == TABLE_ROW % 8, rows_ref[TABLE_ROW - 4 : TABLE_ROW + 4, :], 0.0)
        for part in range(2):
            weight = zero
            for i in range(6):
                weight = jnp.where(lane == 6 * part + i, float(8**i), weight)
            code = jnp.sum(entries * weight).astype(jnp.int32)
            for i in range(6):
                table_ref[s * 12 + 6 * part + i] = (code >> (3 * i)) & 7
        return carry

    lax.fori_loop(0, STEPS, unpack, 0)
    for i in range(STEPS * 3):
        for v in range(2 * (OWN_HI - OWN_LO)):
            grad_ref[i, v] = zero

    def next_z(a, b):
        u, w = pltpu.roll(a, 7, 0), pltpu.roll(b, 7, 0)
        return jnp.where(last, w, u), jnp.where(last, zero, w)

    def prev_z(a, b):
        u, w = pltpu.roll(a, 1, 0), pltpu.roll(b, 1, 0)
        return jnp.where(first, zero, u), jnp.where(first, u, w)

    def put(vectors, row):
        for zo in range(2):
            for gg in range(4):
                value = jnp.where(
                    even,
                    pltpu.roll(vectors[zo, 2 * gg], 128 - HALO, 1),
                    pltpu.roll(vectors[zo, 2 * gg + 1], HALO, 1),
                )
                out_ref[pl.ds(row + 8 * OUT_ROWS * zo + gg, 8, stride=OUT_ROWS), :] = value

    def one_pair(p, carry):
        owner = p // 2
        base = owner * 12
        one = p % 2
        start = table_ref[base + 2 * one]
        target = table_ref[base + 2 * one + 1]
        steps = [table_ref[base + 4 + 4 * one + k] for k in range(WIN)]
        out_row = owner * (NZ * OUT_ROWS) + 4 * one

        def state(k, i):
            return snap_ref[start, i] if k == 0 else rho_ref[k - 1, i]

        for k in range(WIN):
            step = steps[k]
            lo, hi = (0, GROUPS) if k < WIN - 1 else (1, GROUPS - 1)
            mids, ups, downs = {}, {}, {}
            finals = {}
            for g in range(GROUPS + 1):
                if g < GROUPS:
                    wp, wm, mid = [], [], []
                    for zo in range(2):
                        i = zo * GROUPS + g
                        rho = state(k, i)
                        spread = near * rho
                        hx = drift_ref[step, 0, i] * rho
                        hy = drift_ref[step, 1, i] * rho
                        hz = drift_ref[step, 2, i] * rho
                        downs[zo, g] = pltpu.roll(spread - hy, 128 - PITCH, 1)
                        ups[zo, g] = pltpu.roll(spread + hy, PITCH, 1)
                        mid.append(keep * rho + pltpu.roll(spread - hx, 127, 1) + pltpu.roll(spread + hx, 1, 1))
                        wp.append(spread + hz)
                        wm.append(spread - hz)
                    n = next_z(*wm)
                    q = prev_z(*wp)
                    for zo in range(2):
                        mids[zo, g] = mid[zo] + n[zo] + q[zo]
                d = g - 1
                if d >= lo and d < hi:
                    for zo in range(2):
                        after = downs[zo, min(d + 1, GROUPS - 1)]
                        before = ups[zo, max(d - 1, 0)]
                        value = mids[zo, d] + jnp.where(low, downs[zo, d], after) + jnp.where(high, ups[zo, d], before)
                        i = zo * GROUPS + d
                        if k < WIN - 1:
                            rho_ref[k, i] = value
                        else:
                            lam_ref[0, i] = value - snap_ref[target, i]
                            finals[zo, d - OWN_LO] = value
            if k == WIN - 1:
                put(finals, out_row)

        for index in range(WIN):
            k = WIN - 1 - index
            step = steps[k]
            source, sink = index % 2, 1 - index % 2
            lo, hi = (1, GROUPS - 1) if index < WIN - 1 else (OWN_LO, OWN_HI)
            fields, ups, downs = {}, {}, {}
            finals = {}
            for g in range(1, GROUPS):
                if g < GROUPS - 1:
                    for zo in range(2):
                        lam = lam_ref[source, zo * GROUPS + g]
                        fields[zo, g] = lam
                        downs[zo, g] = pltpu.roll(lam, 128 - PITCH, 1)
                        ups[zo, g] = pltpu.roll(lam, PITCH, 1)
                d = g - 1
                if d >= lo and d < hi:
                    n = next_z(fields[0, d], fields[1, d])
                    q = prev_z(fields[0, d], fields[1, d])
                    for zo in range(2):
                        i = zo * GROUPS + d
                        lam = fields[zo, d]
                        xp, xm = pltpu.roll(lam, 127, 1), pltpu.roll(lam, 1, 1)
                        yp = jnp.where(low, downs[zo, d], downs[zo, min(d + 1, GROUPS - 2)])
                        ym = jnp.where(high, ups[zo, d], ups[zo, max(d - 1, 1)])
                        dx, dy, dz = xp - xm, yp - ym, n[zo] - q[zo]
                        total = (xp + xm) + (yp + ym) + (n[zo] + q[zo])
                        value = (
                            keep * lam
                            + near * total
                            + drift_ref[step, 0, i] * dx
                            + drift_ref[step, 1, i] * dy
                            + drift_ref[step, 2, i] * dz
                        )
                        if index < WIN - 1:
                            lam_ref[sink, i] = value
                        else:
                            finals[zo, d - OWN_LO] = value
                        if OWN_LO <= d < OWN_HI:
                            weight = half * state(k, i)
                            v = zo * (OWN_HI - OWN_LO) + d - OWN_LO
                            for c, slope in enumerate((dx, dy, dz)):
                                grad_ref[step * 3 + c, v] += weight * slope
            if index == WIN - 1:
                put(finals, out_row + 8)
        return carry

    lax.fori_loop(0, PAIRS, one_pair, 0)

    def store_grads(s, carry):
        for c in range(3):
            own = {
                (zo, g): grad_ref[s * 3 + c, zo * (OWN_HI - OWN_LO) + g]
                for zo in range(2)
                for g in range(OWN_HI - OWN_LO)
            }
            put(own, s * (NZ * OUT_ROWS) + 16 + 4 * c)
        return carry

    lax.fori_loop(0, STEPS, store_grads, 0)


def planes_kernel(in_ref, final_ref, adjoint_ref, grad_ref, plane_ref):
    block = lanes() // OWN_X

    def rows_of(by, carry):
        for t in range(4):
            for h in range(2):
                v = [in_ref[by * 16 + 8 * h + a, 8 * t : 8 * t + 8, :] for a in range(8)]
                for bit in (1, 2, 4):
                    clear = (block & bit) == 0
                    for a in range(8):
                        if not a & bit:
                            u, w = v[a], v[a | bit]
                            v[a] = jnp.where(clear, u, pltpu.roll(w, 16 * bit, 1))
                            v[a | bit] = jnp.where(clear, pltpu.roll(u, 128 - 16 * bit, 1), w)
                for q in range(8):
                    row = 4 * (q % 2) + q // 2
                    plane_ref[2 * t, h, pl.ds(row, 4, stride=8), :] = v[q][0:4]
                    if t < 3:
                        plane_ref[2 * t + 1, h, pl.ds(row, 4, stride=8), :] = v[q][4:8]
        at = pl.multiple_of(by * OWN_Y, OWN_Y)
        for h in range(2):
            cols = slice(128 * h, 128 * h + 128)
            for i in range(2):
                final_ref[i, 0, pl.ds(at, OWN_Y), cols] = plane_ref[i, h]
                adjoint_ref[i, 0, pl.ds(at, OWN_Y), cols] = plane_ref[2 + i, h]
            for c in range(3):
                grad_ref[0, c, 0, pl.ds(at, OWN_Y), cols] = plane_ref[4 + c, h]
        return carry

    lax.fori_loop(0, 8, rows_of, 0)


def local(snapshots, drift, pair_table, plan):
    f32, bf16 = jnp.float32, jnp.bfloat16
    smem = pl.BlockSpec(memory_space=pltpu.SMEM)
    vmem = pl.BlockSpec(memory_space=pltpu.VMEM)
    windows = pl.pallas_call(
        build_kernel,
        out_shape=jax.ShapeDtypeStruct((128, IN_ROWS, 128), bf16),
        in_specs=[smem, smem, vmem, vmem],
        out_specs=vmem,
        scratch_shapes=[pltpu.VMEM((4, 2, 288, 128), f32), pltpu.VMEM((5, 72, 128), f32)],
    )(pair_table, plan, snapshots, drift)
    windows = lax.all_to_all(windows, ("step", "space"), 0, 0, tiled=True)
    groups = 2 * GROUPS
    results = pl.pallas_call(
        window_kernel,
        out_shape=jax.ShapeDtypeStruct((128 * OUT_ROWS, 128), f32),
        in_specs=[vmem],
        out_specs=vmem,
        scratch_shapes=[
            pltpu.VMEM((NZ * IN_ROWS, 128), f32),
            pltpu.VMEM((STEPS, groups) + VREG, f32),
            pltpu.VMEM((STEPS, 3, groups) + VREG, f32),
            pltpu.VMEM((WIN - 1, groups) + VREG, f32),
            pltpu.VMEM((2, groups) + VREG, f32),
            pltpu.VMEM((STEPS * 3, 2 * (OWN_HI - OWN_LO)) + VREG, f32),
            pltpu.SMEM((STEPS * 12,), jnp.int32),
        ],
    )(windows)
    results = results.reshape(128, OUT_ROWS, 128)
    results = lax.all_to_all(results, ("step", "space"), 0, 0, tiled=True)
    return pl.pallas_call(
        planes_kernel,
        out_shape=(
            jax.ShapeDtypeStruct((2, 1, SIDE, SIDE), f32),
            jax.ShapeDtypeStruct((2, 1, SIDE, SIDE), f32),
            jax.ShapeDtypeStruct((1, 3, 1, SIDE, SIDE), f32),
        ),
        in_specs=[vmem],
        out_specs=(vmem, vmem, vmem),
        scratch_shapes=[pltpu.VMEM((7, 2, OWN_Y, 128), f32)],
    )(results)


def solution(mesh):
    return jax.shard_map(
        local,
        mesh=mesh,
        in_specs=(
            P("step", "space", None, None),
            P("step", None, "space", None, None),
            P("step", None),
            P("step", None),
        ),
        out_specs=(
            P("step", "space", None, None),
            P("step", "space", None, None),
            P("step", None, "space", None, None),
        ),
        check_vma=False,
    )
```

```python
import jax
import jax.numpy as jnp
from jax import lax
from jax.experimental import pallas as pl
from jax.experimental.pallas import tpu as pltpu
from jax.sharding import PartitionSpec as P

WIN = 4
NZ = 16
SIDE = 256
PAIRS = 16
STEPS = 8
OWN_Y = 32
OWN_X = 16
HALO = 2 * WIN
PITCH = OWN_X + 2 * HALO
OWN = 8
GROUPS = 12
IN_ROWS = 64
OUT_ROWS = 28
VREG = (8, 128)

time_step = 0.1
diffusion = 1.0
near = time_step * diffusion
keep = 1.0 - 6.0 * near
half = 0.5 * time_step


def lanes():
    return lax.broadcasted_iota(jnp.int32, VREG, 1)


def subs():
    return lax.broadcasted_iota(jnp.int32, VREG, 0)


def spread_of(sign):
    return jnp.exp2(((lanes() * 37) % 128).astype(jnp.float32) * (sign / 128.0))


def swap(u, w, clear, width):
    return jnp.where(clear, u, pltpu.roll(w, width, 1)), jnp.where(clear, pltpu.roll(u, 128 - width, 1), w)


def build_kernel(pairs_ref, plan_ref, snap_ref, drift_ref, out_ref, tile_ref):
    lane = lanes()
    block = lane // PITCH
    one, two = (block & 1) == 0, (block & 2) == 0
    wrap = lane < 112
    outer = (block == 0) | (block == 3)
    table = jnp.zeros(VREG, jnp.float32)
    for i in range(12):
        entry = pairs_ref[i // 2, i % 2] if i < 4 else plan_ref[(i - 4) // 4, (i - 4) % 4]
        table = jnp.where(lane == PITCH + i, entry.astype(jnp.float32), table)

    def tiles(by, carry):
        at = pl.multiple_of(32 * by, 32)
        for f in range(4):
            even, odd = {}, {}
            for j in range(4):
                rows = pl.ds(at + 8 * j, 8)
                if f == 0:
                    parts = [snap_ref[0, 0, rows, 128 * h : 128 * h + 128] for h in range(2)]
                else:
                    parts = [
                        drift_ref[0, f - 1, 0, rows, 128 * h : 128 * h + 128].astype(jnp.float32) for h in range(2)
                    ]
                moved = [pltpu.roll(part, 112, 1) for part in parts]
                for h in range(2):
                    even[h, j] = parts[h]
                    odd[h, j] = jnp.where(wrap, moved[h], moved[1 - h])
            for h in range(2):
                for parity, source in enumerate((even, odd)):
                    v = [source[h, j] for j in range(4)]
                    v[0], v[1] = swap(v[0], v[1], one, PITCH)
                    v[2], v[3] = swap(v[2], v[3], one, PITCH)
                    v[0], v[2] = swap(v[0], v[2], two, 2 * PITCH)
                    v[1], v[3] = swap(v[1], v[3], two, 2 * PITCH)
                    for b in range(4):
                        bx = 8 * h + 2 * b + parity
                        tile_ref[f, bx, pl.ds(pl.multiple_of(8 * by, 8), 8), :] = v[b]
        return carry

    lax.fori_loop(0, 8, tiles, 0)

    def messages(bx, carry):
        for by in range(8):
            own, rim = [], []
            for f in range(4):
                tile = tile_ref[f, bx, 8 * by : 8 * by + 8, :]
                below = (8 * by + 8) % 64
                above = (8 * by - 8) % 64
                edge = jnp.where(
                    block == 0, tile_ref[f, bx, below : below + 8, :], tile_ref[f, bx, above : above + 8, :]
                )
                if f == 0:
                    for values, value in ((own, tile), (rim, edge)):
                        high = value.astype(jnp.bfloat16).astype(jnp.float32)
                        values += [high, value - high]
                else:
                    own.append(tile)
                    rim.append(edge)
            ends = [
                jnp.where(outer, rim[0], pltpu.roll(rim[1], 64, 1)),
                jnp.where(outer, rim[2], pltpu.roll(rim[3], 64, 1)),
                jnp.where(outer, rim[4], table),
            ]
            out_ref[by * 16 + bx] = jnp.concatenate(own + ends, axis=0).astype(jnp.bfloat16)
        return carry

    lax.fori_loop(0, 16, messages, 0)


PLANE_ROWS = 65


def window_kernel(in_ref, out_ref, rows_ref, snap_ref, drift_ref, rho_ref, lam_ref, grad_ref, table_ref):
    lane = lanes()
    sub = subs()
    zero = jnp.zeros(VREG, jnp.float32)
    first, last = sub == 0, sub == 7
    block = lane // PITCH
    is0, is3 = block == 0, block == 3
    outer = is0 | is3
    mine = (lane % PITCH >= HALO) & (lane % PITCH < HALO + OWN_X)

    def unpack(s, carry):
        for z in range(NZ):
            rows_ref[PLANE_ROWS * z : PLANE_ROWS * z + IN_ROWS, :] = in_ref[s * NZ + z].astype(jnp.float32)
        for zo in range(2):

            def row(r):
                return rows_ref[pl.ds(PLANE_ROWS * zo + r, 8, stride=2 * PLANE_ROWS), :]

            for g in range(GROUPS):
                if g < OWN:
                    parts = [row(8 * f + g) for f in range(5)]
                else:
                    e = g - OWN
                    parts = []
                    for t in range(3):
                        a, b = row(40 + 8 * t + e), row(44 + 8 * t + e)
                        direct, across = jnp.where(is0, a, b), jnp.where(is0, b, a)
                        parts.append(jnp.where(outer, direct, pltpu.roll(across, 64, 1)))
                        if t < 2:
                            direct, across = jnp.where(block == 1, a, b), jnp.where(block == 1, b, a)
                            parts.append(jnp.where(outer, pltpu.roll(across, 64, 1), direct))
                snap_ref[s, zo * GROUPS + g] = parts[0] + parts[1]
                for c in range(3):
                    drift_ref[s, c, zo * GROUPS + g] = near + half * parts[2 + c]
        entries = rows_ref[56:57, :]
        at = lax.broadcasted_iota(jnp.int32, (1, 128), 1) - PITCH
        for part in range(2):
            weight = jnp.zeros((1, 128), jnp.float32)
            for i in range(6):
                weight = jnp.where(at == 6 * part + i, float(8**i), weight)
            code = jnp.sum(entries * weight).astype(jnp.int32)
            for i in range(6):
                table_ref[s * 12 + 6 * part + i] = (code >> (3 * i)) & 7
        return carry

    lax.fori_loop(0, STEPS, unpack, 0)

    def clear(i, carry):
        for v in range(2 * OWN):
            grad_ref[i, v] = zero
        return carry

    lax.fori_loop(0, STEPS * 3, clear, 0)

    scale = spread_of(1.0)

    def put(vectors, row, factor):
        for zo in range(2):
            for gg in range(4):
                value = jnp.where(mine, vectors[zo, 2 * gg], pltpu.roll(vectors[zo, 2 * gg + 1], OWN_X, 1))
                out_ref[pl.ds(row + OUT_ROWS * zo + gg, 8, stride=2 * OUT_ROWS), :] = value * factor

    def from_below(g, zo, v):
        if g == 7:
            return pltpu.roll(jnp.where(is0, v[zo, 8], v[zo, 0]), 96, 1)
        if g == 11:
            return jnp.where(is3, pltpu.roll(v[zo, 0], 96, 1), pltpu.roll(v[zo, 8], 64, 1))
        return v[zo, g + 1]

    def from_above(g, zo, v):
        if g == 0:
            return pltpu.roll(jnp.where(is3, v[zo, 11], v[zo, 7]), 32, 1)
        if g == 8:
            return jnp.where(is0, pltpu.roll(v[zo, 7], 32, 1), pltpu.roll(v[zo, 11], 64, 1))
        return v[zo, g - 1]

    needs = {g: {g, g + 1, g - 1} for g in range(GROUPS)}
    needs[0] = {0, 1, 7, 11}
    needs[7] = {7, 6, 0, 8}
    needs[8] = {8, 9, 7, 11}
    needs[11] = {11, 10, 0, 8}
    order = (7, 11, 8, 0, 1, 2, 3, 4, 5, 6, 9, 10)

    def one_pair(p, carry):
        owner = p // 2
        base = owner * 12
        which = p % 2
        start = table_ref[base + 2 * which]
        target = table_ref[base + 2 * which + 1]
        steps = [table_ref[base + 4 + 4 * which + k] for k in range(WIN)]
        out_row = owner * (NZ * OUT_ROWS) + 4 * which

        def state(k, i):
            return snap_ref[start, i] if k == 0 else rho_ref[k - 1, i]

        for k in range(WIN):
            step = steps[k]
            mids, ups, downs, finals = {}, {}, {}, {}
            done, todo = set(), list(order)
            for g in order:
                zp, zm = [], []
                for zo in range(2):
                    i = zo * GROUPS + g
                    rho = state(k, i)
                    both = (2.0 * near) * rho
                    xp = drift_ref[step, 0, i] * rho
                    yp = drift_ref[step, 1, i] * rho
                    zp.append(drift_ref[step, 2, i] * rho)
                    zm.append(both - zp[zo])
                    downs[zo, g] = both - yp
                    ups[zo, g] = yp
                    mids[zo, g] = keep * rho + (pltpu.roll(both - xp, 127, 1) + pltpu.roll(xp, 1, 1))
                mids[0, g] += zm[1] + jnp.where(first, zero, pltpu.roll(zp[1], 1, 0))
                mids[1, g] += zp[0] + jnp.where(last, zero, pltpu.roll(zm[0], 7, 0))
                done.add(g)
                for d in [d for d in todo if needs[d] & set(order) <= done]:
                    todo.remove(d)
                    for zo in range(2):
                        value = mids[zo, d] + (from_below(d, zo, downs) + from_above(d, zo, ups))
                        i = zo * GROUPS + d
                        if k < WIN - 1:
                            rho_ref[k, i] = value
                        else:
                            lam_ref[0, i] = value - snap_ref[target, i]
                            finals[zo, d] = value
            if k == WIN - 1:
                put(finals, out_row, scale)

        for index in range(WIN):
            k = WIN - 1 - index
            step = steps[k]
            source, sink = index % 2, 1 - index % 2
            wanted = [g for g in order if g < OWN or index < 2 or (index == 2 and g in (8, 11))]
            fields, finals = {}, {}
            done, todo = set(), list(wanted)
            for g in [g for g in order if index < 3 or g not in (9, 10)]:
                for zo in range(2):
                    fields[zo, g] = lam_ref[source, zo * GROUPS + g]
                done.add(g)
                for d in [d for d in todo if needs[d] & set(order) <= done]:
                    todo.remove(d)
                    zn = fields[1, d], jnp.where(last, zero, pltpu.roll(fields[0, d], 7, 0))
                    zq = jnp.where(first, zero, pltpu.roll(fields[1, d], 1, 0)), fields[0, d]
                    for zo in range(2):
                        i = zo * GROUPS + d
                        lam = fields[zo, d]
                        xn, xq = pltpu.roll(lam, 127, 1), pltpu.roll(lam, 1, 1)
                        yn, yq = from_below(d, zo, fields), from_above(d, zo, fields)
                        dx, dy, dz = xn - xq, yn - yq, zn[zo] - zq[zo]
                        value = (
                            (keep * lam + (2.0 * near) * (xq + yq + zq[zo]))
                            + (drift_ref[step, 0, i] * dx + drift_ref[step, 1, i] * dy)
                            + drift_ref[step, 2, i] * dz
                        )
                        if index < WIN - 1:
                            lam_ref[sink, i] = value
                        else:
                            finals[zo, d] = value
                        if d < OWN:
                            rho = state(k, i)
                            for c, slope in enumerate((dx, dy, dz)):
                                grad_ref[step * 3 + c, zo * OWN + d] += rho * slope
            if index == WIN - 1:
                put(finals, out_row + 8, scale)
        return carry

    lax.fori_loop(0, PAIRS, one_pair, 0)

    def store_grads(s, carry):
        for c in range(3):
            own = {(zo, g): grad_ref[s * 3 + c, zo * OWN + g] for zo in range(2) for g in range(OWN)}
            put(own, s * (NZ * OUT_ROWS) + 16 + 4 * c, half * scale)
        return carry

    lax.fori_loop(0, STEPS, store_grads, 0)


def planes_kernel(in_ref, final_ref, adjoint_ref, grad_ref, plane_ref):
    lane = lanes()
    block = ((lane + 120) % 128) // OWN_X
    clear = {bit: (block & bit) == 0 for bit in (1, 2, 4)}
    inverse = spread_of(-1.0)
    carried = lane < HALO

    def rows_of(by, carry):
        for t in range(4):
            start = 8 * t if t < 3 else 20
            sides = []
            for h in range(2):
                v = [in_ref[pl.ds((by * 16 + 8 * h + a) * OUT_ROWS + start, 8), :] * inverse for a in range(8)]
                for bit in (1, 2, 4):
                    for a in range(8):
                        if not a & bit:
                            v[a], v[a | bit] = swap(v[a], v[a | bit], clear[bit], OWN_X * bit)
                sides.append(v)
            for h in range(2):
                for q in range(8):
                    value = jnp.where(carried, sides[1 - h][q], sides[h][q])
                    rows = pl.ds(8 * (q // 2) + q % 2, 4, stride=2)
                    if t < 3:
                        plane_ref[2 * t, h, rows, :] = value[0:4]
                        plane_ref[2 * t + 1, h, rows, :] = value[4:8]
                    else:
                        plane_ref[6, h, rows, :] = value[4:8]
        at = pl.multiple_of(by * OWN_Y, OWN_Y)
        for h in range(2):
            cols = slice(128 * h, 128 * h + 128)
            for i in range(2):
                final_ref[i, 0, pl.ds(at, OWN_Y), cols] = plane_ref[i, h]
                adjoint_ref[i, 0, pl.ds(at, OWN_Y), cols] = plane_ref[2 + i, h]
            for c in range(3):
                grad_ref[0, c, 0, pl.ds(at, OWN_Y), cols] = plane_ref[4 + c, h]
        return carry

    lax.fori_loop(0, 8, rows_of, 0)


def local(snapshots, drift, pair_table, plan):
    f32, bf16, f16 = jnp.float32, jnp.bfloat16, jnp.float16
    smem = pl.BlockSpec(memory_space=pltpu.SMEM)
    vmem = pl.BlockSpec(memory_space=pltpu.VMEM)
    windows = pl.pallas_call(
        build_kernel,
        out_shape=jax.ShapeDtypeStruct((128, IN_ROWS, 128), bf16),
        in_specs=[smem, smem, vmem, vmem],
        out_specs=vmem,
        scratch_shapes=[pltpu.VMEM((4, 16, 64, 128), f32)],
    )(pair_table, plan, snapshots, drift)
    windows = lax.all_to_all(windows, ("step", "space"), 0, 0, tiled=True)
    groups = 2 * GROUPS
    results = pl.pallas_call(
        window_kernel,
        out_shape=jax.ShapeDtypeStruct((128 * OUT_ROWS, 128), f32),
        in_specs=[vmem],
        out_specs=vmem,
        scratch_shapes=[
            pltpu.VMEM((NZ * PLANE_ROWS, 128), f32),
            pltpu.VMEM((STEPS, groups) + VREG, f32),
            pltpu.VMEM((STEPS, 3, groups) + VREG, f32),
            pltpu.VMEM((WIN - 1, groups) + VREG, f32),
            pltpu.VMEM((2, groups) + VREG, f32),
            pltpu.VMEM((STEPS * 3, 2 * OWN) + VREG, f32),
            pltpu.SMEM((STEPS * 12,), jnp.int32),
        ],
    )(windows)
    results = results.reshape(128, OUT_ROWS // 4, 4, 128).astype(f16)
    results = lax.all_to_all(results, ("step", "space"), 0, 0, tiled=True)
    results = results.astype(f32).reshape(128 * OUT_ROWS, 128)
    return pl.pallas_call(
        planes_kernel,
        out_shape=(
            jax.ShapeDtypeStruct((2, 1, SIDE, SIDE), f32),
            jax.ShapeDtypeStruct((2, 1, SIDE, SIDE), f32),
            jax.ShapeDtypeStruct((1, 3, 1, SIDE, SIDE), f32),
        ),
        in_specs=[vmem],
        out_specs=(vmem, vmem, vmem),
        scratch_shapes=[pltpu.VMEM((7, 2, OWN_Y, 128), f32)],
    )(results)


def solution(mesh):
    return jax.shard_map(
        local,
        mesh=mesh,
        in_specs=(
            P("step", "space", None, None),
            P("step", None, "space", None, None),
            P("step", None),
            P("step", None),
        ),
        out_specs=(
            P("step", "space", None, None),
            P("step", "space", None, None),
            P("step", None, "space", None, None),
        ),
        check_vma=False,
    )
```

```python
import jax
import jax.numpy as jnp
from jax import lax
from jax.experimental import pallas as pl
from jax.experimental.pallas import tpu as pltpu
from jax.sharding import PartitionSpec as P

WIN = 4
NZ = 16
SIDE = 256
PAIRS = 16
STEPS = 8
TOGETHER = 2
OWN_Y = 32
OWN_X = 16
HALO = 2 * WIN
PITCH = OWN_X + 2 * HALO
OWN = 8
GROUPS = 12
IN_ROWS = 64
OUT_ROWS = 28
VREG = (8, 128)

time_step = 0.1
diffusion = 1.0
near = time_step * diffusion
keep = 1.0 - 6.0 * near
half = 0.5 * time_step


def lanes():
    return lax.broadcasted_iota(jnp.int32, VREG, 1)


def subs():
    return lax.broadcasted_iota(jnp.int32, VREG, 0)


def spread_of(sign):
    return jnp.exp2(((lanes() * 37) % 128).astype(jnp.float32) * (sign / 128.0))


def swap(u, w, clear, width):
    return jnp.where(clear, u, pltpu.roll(w, width, 1)), jnp.where(clear, pltpu.roll(u, 128 - width, 1), w)


def build_kernel(pairs_ref, plan_ref, snap_ref, drift_ref, out_ref, tile_ref):
    lane = lanes()
    block = lane // PITCH
    one, two = (block & 1) == 0, (block & 2) == 0
    wrap = lane < 112
    outer = (block == 0) | (block == 3)
    table = jnp.zeros(VREG, jnp.float32)
    for i in range(12):
        entry = pairs_ref[i // 2, i % 2] if i < 4 else plan_ref[(i - 4) // 4, (i - 4) % 4]
        table = jnp.where(lane == PITCH + i, entry.astype(jnp.float32), table)

    def tiles(by, carry):
        at = pl.multiple_of(32 * by, 32)
        for f in range(4):
            even, odd = {}, {}
            for j in range(4):
                rows = pl.ds(at + 8 * j, 8)
                if f == 0:
                    parts = [snap_ref[0, 0, rows, 128 * h : 128 * h + 128] for h in range(2)]
                else:
                    parts = [
                        drift_ref[0, f - 1, 0, rows, 128 * h : 128 * h + 128].astype(jnp.float32) for h in range(2)
                    ]
                moved = [pltpu.roll(part, 112, 1) for part in parts]
                for h in range(2):
                    even[h, j] = parts[h]
                    odd[h, j] = jnp.where(wrap, moved[h], moved[1 - h])
            for h in range(2):
                for parity, source in enumerate((even, odd)):
                    v = [source[h, j] for j in range(4)]
                    v[0], v[1] = swap(v[0], v[1], one, PITCH)
                    v[2], v[3] = swap(v[2], v[3], one, PITCH)
                    v[0], v[2] = swap(v[0], v[2], two, 2 * PITCH)
                    v[1], v[3] = swap(v[1], v[3], two, 2 * PITCH)
                    for b in range(4):
                        bx = 8 * h + 2 * b + parity
                        tile_ref[f, bx, pl.ds(pl.multiple_of(8 * by, 8), 8), :] = v[b]
        return carry

    lax.fori_loop(0, 8, tiles, 0)

    def messages(bx, carry):
        for by in range(8):
            own, rim = [], []
            for f in range(4):
                tile = tile_ref[f, bx, 8 * by : 8 * by + 8, :]
                below = (8 * by + 8) % 64
                above = (8 * by - 8) % 64
                edge = jnp.where(
                    block == 0, tile_ref[f, bx, below : below + 8, :], tile_ref[f, bx, above : above + 8, :]
                )
                if f == 0:
                    for values, value in ((own, tile), (rim, edge)):
                        high = value.astype(jnp.bfloat16).astype(jnp.float32)
                        values += [high, value - high]
                else:
                    own.append(tile)
                    rim.append(edge)
            ends = [
                jnp.where(outer, rim[0], pltpu.roll(rim[1], 64, 1)),
                jnp.where(outer, rim[2], pltpu.roll(rim[3], 64, 1)),
                jnp.where(outer, rim[4], table),
            ]
            out_ref[by * 16 + bx] = jnp.concatenate(own + ends, axis=0).astype(jnp.bfloat16)
        return carry

    lax.fori_loop(0, 16, messages, 0)


PLANE_ROWS = 65


def window_kernel(in_ref, out_ref, rows_ref, snap_ref, drift_ref, rho_ref, lam_ref, grad_ref, table_ref):
    lane = lanes()
    sub = subs()
    zero = jnp.zeros(VREG, jnp.float32)
    first, last = sub == 0, sub == 7
    block = lane // PITCH
    is0, is3 = block == 0, block == 3
    outer = is0 | is3
    mine = (lane % PITCH >= HALO) & (lane % PITCH < HALO + OWN_X)

    def unpack(s, carry):
        for z in range(NZ):
            rows_ref[PLANE_ROWS * z : PLANE_ROWS * z + IN_ROWS, :] = in_ref[s * NZ + z].astype(jnp.float32)
        for zo in range(2):

            def row(r):
                return rows_ref[pl.ds(PLANE_ROWS * zo + r, 8, stride=2 * PLANE_ROWS), :]

            for g in range(GROUPS):
                if g < OWN:
                    parts = [row(8 * f + g) for f in range(5)]
                else:
                    e = g - OWN
                    parts = []
                    for t in range(3):
                        a, b = row(40 + 8 * t + e), row(44 + 8 * t + e)
                        direct, across = jnp.where(is0, a, b), jnp.where(is0, b, a)
                        parts.append(jnp.where(outer, direct, pltpu.roll(across, 64, 1)))
                        if t < 2:
                            direct, across = jnp.where(block == 1, a, b), jnp.where(block == 1, b, a)
                            parts.append(jnp.where(outer, pltpu.roll(across, 64, 1), direct))
                snap_ref[s, zo * GROUPS + g] = parts[0] + parts[1]
                for c in range(3):
                    drift_ref[s, c, zo * GROUPS + g] = near + half * parts[2 + c]
        entries = rows_ref[56:57, :]
        at = lax.broadcasted_iota(jnp.int32, (1, 128), 1) - PITCH
        for part in range(2):
            weight = jnp.zeros((1, 128), jnp.float32)
            for i in range(6):
                weight = jnp.where(at == 6 * part + i, float(8**i), weight)
            code = jnp.sum(entries * weight).astype(jnp.int32)
            for i in range(6):
                table_ref[s * 12 + 6 * part + i] = (code >> (3 * i)) & 7
        return carry

    lax.fori_loop(0, STEPS, unpack, 0)

    def clear(i, carry):
        for v in range(2 * OWN):
            grad_ref[i, v] = zero
        return carry

    lax.fori_loop(0, STEPS * 3, clear, 0)

    scale = spread_of(1.0)

    def put_pair(vectors, zo, g, row, factor):
        even, odd = (zo, g - g % 2), (zo, g - g % 2 + 1)
        if g < OWN and even in vectors and odd in vectors:
            value = jnp.where(mine, vectors[even], pltpu.roll(vectors[odd], OWN_X, 1))
            out_ref[pl.ds(row + OUT_ROWS * zo + g // 2, 8, stride=2 * OUT_ROWS), :] = value * factor

    def from_below(g, zo, v):
        if g == 7:
            return pltpu.roll(jnp.where(is0, v[zo, 8], v[zo, 0]), 96, 1)
        if g == 11:
            return jnp.where(is3, pltpu.roll(v[zo, 0], 96, 1), pltpu.roll(v[zo, 8], 64, 1))
        return v[zo, g + 1]

    def from_above(g, zo, v):
        if g == 0:
            return pltpu.roll(jnp.where(is3, v[zo, 11], v[zo, 7]), 32, 1)
        if g == 8:
            return jnp.where(is0, pltpu.roll(v[zo, 7], 32, 1), pltpu.roll(v[zo, 11], 64, 1))
        return v[zo, g - 1]

    needs = {g: {g, g + 1, g - 1} for g in range(GROUPS)}
    needs[0] = {0, 1, 7, 11}
    needs[7] = {7, 6, 0, 8}
    needs[8] = {8, 9, 7, 11}
    needs[11] = {11, 10, 0, 8}
    order = (7, 11, 8, 0, 1, 2, 3, 4, 5, 6, 9, 10)

    def forward(c, k):
        step = c["steps"][k]
        mids, ups, downs, finals = {}, {}, {}, {}
        done, todo = set(), list(order)
        for g in order:
            zp, zm = [], []
            for zo in range(2):
                i = zo * GROUPS + g
                rho = c["state"](k, i)
                both = (2.0 * near) * rho
                xp = drift_ref[step, 0, i] * rho
                yp = drift_ref[step, 1, i] * rho
                zp.append(drift_ref[step, 2, i] * rho)
                zm.append(both - zp[zo])
                downs[zo, g] = both - yp
                ups[zo, g] = yp
                mids[zo, g] = keep * rho + (pltpu.roll(both - xp, 127, 1) + pltpu.roll(xp, 1, 1))
            mids[0, g] += zm[1] + jnp.where(first, zero, pltpu.roll(zp[1], 1, 0))
            mids[1, g] += zp[0] + jnp.where(last, zero, pltpu.roll(zm[0], 7, 0))
            done.add(g)
            for d in [d for d in todo if needs[d] & set(order) <= done]:
                todo.remove(d)
                for zo in range(2):
                    value = mids[zo, d] + (from_below(d, zo, downs) + from_above(d, zo, ups))
                    i = zo * GROUPS + d
                    if k < WIN - 1:
                        c["rho"][k, i] = value
                    else:
                        c["lam"][0, i] = value - snap_ref[c["target"], i]
                        finals[zo, d] = value
                    if k == WIN - 1:
                        put_pair(finals, zo, d, c["row"], scale)

    def backward(c, index):
        k = WIN - 1 - index
        step = c["steps"][k]
        source, sink = index % 2, 1 - index % 2
        wanted = [g for g in order if g < OWN or index < 2 or (index == 2 and g in (8, 11))]
        fields, finals = {}, {}
        done, todo = set(), list(wanted)
        for g in [g for g in order if index < 3 or g not in (9, 10)]:
            for zo in range(2):
                fields[zo, g] = c["lam"][source, zo * GROUPS + g]
            done.add(g)
            for d in [d for d in todo if needs[d] & set(order) <= done]:
                todo.remove(d)
                zn = fields[1, d], jnp.where(last, zero, pltpu.roll(fields[0, d], 7, 0))
                zq = jnp.where(first, zero, pltpu.roll(fields[1, d], 1, 0)), fields[0, d]
                for zo in range(2):
                    i = zo * GROUPS + d
                    lam = fields[zo, d]
                    xn, xq = pltpu.roll(lam, 127, 1), pltpu.roll(lam, 1, 1)
                    yn, yq = from_below(d, zo, fields), from_above(d, zo, fields)
                    dx, dy, dz = xn - xq, yn - yq, zn[zo] - zq[zo]
                    value = (
                        (keep * lam + (2.0 * near) * (xq + yq + zq[zo]))
                        + (drift_ref[step, 0, i] * dx + drift_ref[step, 1, i] * dy)
                        + drift_ref[step, 2, i] * dz
                    )
                    if index < WIN - 1:
                        c["lam"][sink, i] = value
                    else:
                        finals[zo, d] = value
                        put_pair(finals, zo, d, c["row"] + 8, scale)
                    if d < OWN:
                        rho = c["state"](k, i)
                        for n, slope in enumerate((dx, dy, dz)):
                            grad_ref[step * 3 + n, zo * OWN + d] += rho * slope

    def pairs_of(i, carry):
        cases = []
        for n in range(TOGETHER):
            p = TOGETHER * i + n
            owner = p // 2
            base = owner * 12
            which = p % 2
            start = table_ref[base + 2 * which]
            rho, lam = rho_ref.at[n], lam_ref.at[n]
            cases.append(
                {
                    "target": table_ref[base + 2 * which + 1],
                    "steps": [table_ref[base + 4 + 4 * which + k] for k in range(WIN)],
                    "row": owner * (NZ * OUT_ROWS) + 4 * which,
                    "rho": rho,
                    "lam": lam,
                    "state": lambda k, i, rho=rho, start=start: snap_ref[start, i] if k == 0 else rho[k - 1, i],
                }
            )
        for k in range(WIN):
            for c in cases:
                forward(c, k)
        for index in range(WIN):
            for c in cases:
                backward(c, index)
        return carry

    lax.fori_loop(0, PAIRS // TOGETHER, pairs_of, 0)

    for s in range(STEPS):
        for c in range(3):
            for zo in range(2):
                own = {(zo, g): grad_ref[s * 3 + c, zo * OWN + g] for g in range(OWN)}
                for g in range(0, OWN, 2):
                    put_pair(own, zo, g, s * (NZ * OUT_ROWS) + 16 + 4 * c, half * scale)


def planes_kernel(in_ref, final_ref, adjoint_ref, grad_ref, plane_ref):
    lane = lanes()
    block = ((lane + 120) % 128) // OWN_X
    clear = {bit: (block & bit) == 0 for bit in (1, 2, 4)}
    inverse = spread_of(-1.0)
    carried = lane < HALO

    def rows_of(by, carry):
        for t in range(4):
            start = 8 * t if t < 3 else 20
            sides = []
            for h in range(2):
                v = [in_ref[pl.ds((by * 16 + 8 * h + a) * OUT_ROWS + start, 8), :] * inverse for a in range(8)]
                for bit in (1, 2, 4):
                    for a in range(8):
                        if not a & bit:
                            v[a], v[a | bit] = swap(v[a], v[a | bit], clear[bit], OWN_X * bit)
                sides.append(v)
            for h in range(2):
                for q in range(8):
                    value = jnp.where(carried, sides[1 - h][q], sides[h][q])
                    rows = pl.ds(8 * (q // 2) + q % 2, 4, stride=2)
                    if t < 3:
                        plane_ref[2 * t, h, rows, :] = value[0:4]
                        plane_ref[2 * t + 1, h, rows, :] = value[4:8]
                    else:
                        plane_ref[6, h, rows, :] = value[4:8]
        at = pl.multiple_of(by * OWN_Y, OWN_Y)
        for h in range(2):
            cols = slice(128 * h, 128 * h + 128)
            for i in range(2):
                final_ref[i, 0, pl.ds(at, OWN_Y), cols] = plane_ref[i, h]
                adjoint_ref[i, 0, pl.ds(at, OWN_Y), cols] = plane_ref[2 + i, h]
            for c in range(3):
                grad_ref[0, c, 0, pl.ds(at, OWN_Y), cols] = plane_ref[4 + c, h]
        return carry

    lax.fori_loop(0, 8, rows_of, 0)


def local(snapshots, drift, pair_table, plan):
    f32, bf16, f16 = jnp.float32, jnp.bfloat16, jnp.float16
    smem = pl.BlockSpec(memory_space=pltpu.SMEM)
    vmem = pl.BlockSpec(memory_space=pltpu.VMEM)
    limit = pltpu.CompilerParams(vmem_limit_bytes=16 << 20)
    windows = pl.pallas_call(
        build_kernel,
        out_shape=jax.ShapeDtypeStruct((128, IN_ROWS, 128), bf16),
        in_specs=[smem, smem, vmem, vmem],
        out_specs=vmem,
        scratch_shapes=[pltpu.VMEM((4, 16, 64, 128), f32)],
        compiler_params=limit,
    )(pair_table, plan, snapshots, drift)
    windows = lax.all_to_all(windows, ("step", "space"), 0, 0, tiled=True)
    groups = 2 * GROUPS
    results = pl.pallas_call(
        window_kernel,
        out_shape=jax.ShapeDtypeStruct((128 * OUT_ROWS, 128), f32),
        in_specs=[vmem],
        out_specs=vmem,
        scratch_shapes=[
            pltpu.VMEM((NZ * PLANE_ROWS, 128), f32),
            pltpu.VMEM((STEPS, groups) + VREG, f32),
            pltpu.VMEM((STEPS, 3, groups) + VREG, f32),
            pltpu.VMEM((TOGETHER, WIN - 1, groups) + VREG, f32),
            pltpu.VMEM((TOGETHER, 2, groups) + VREG, f32),
            pltpu.VMEM((STEPS * 3, 2 * OWN) + VREG, f32),
            pltpu.SMEM((STEPS * 12,), jnp.int32),
        ],
        compiler_params=limit,
    )(windows)
    results = results.reshape(128, OUT_ROWS // 4, 4, 128).astype(f16)
    results = lax.all_to_all(results, ("step", "space"), 0, 0, tiled=True)
    results = results.astype(f32).reshape(128 * OUT_ROWS, 128)
    return pl.pallas_call(
        planes_kernel,
        out_shape=(
            jax.ShapeDtypeStruct((2, 1, SIDE, SIDE), f32),
            jax.ShapeDtypeStruct((2, 1, SIDE, SIDE), f32),
            jax.ShapeDtypeStruct((1, 3, 1, SIDE, SIDE), f32),
        ),
        in_specs=[vmem],
        out_specs=(vmem, vmem, vmem),
        scratch_shapes=[pltpu.VMEM((7, 2, OWN_Y, 128), f32)],
        compiler_params=limit,
    )(results)


def solution(mesh):
    return jax.shard_map(
        local,
        mesh=mesh,
        in_specs=(
            P("step", "space", None, None),
            P("step", None, "space", None, None),
            P("step", None),
            P("step", None),
        ),
        out_specs=(
            P("step", "space", None, None),
            P("step", "space", None, None),
            P("step", None, "space", None, None),
        ),
        check_vma=False,
    )
```
